256 devices in a mesh: node: 4 (over x), table: 64 (over y, z, core).
Axes of the slice: x: 4, y: 4, z: 8, core: 2. Of those that a mesh axis runs over, the one named last changes fastest.
Arguments:
- emb_rows: bfloat16 [131072, 128], P(('node', 'table')), may hold values from -0.23925781 to 0.23925781
- tile_mult: int32 [16384, 128, 128], P(('node', 'table')), may hold values from 0 to 3
- tile_rows: int32 [16384], P(('node', 'table')), may hold values from 0 to 3
- tile_table: int32 [16384], P(('node', 'table')), may hold values from 0 to 63, as said below
- tile_slot: int32 [16384], P(('node', 'table')), may hold values from 0 to 51
- dense: bfloat16 [65536, 128], P(('node', 'table')), may hold values from -6 to 6
- cross_v: bfloat16 [3456, 512], P('node'), may hold values from -0.109375 to 0.109375
- cross_u: bfloat16 [512, 3456], P('node'), may hold values from -0.25 to 0.25
- cross_bias: float32 [3456], replicated, may hold values from -3 to 3
- cotangent: bfloat16 [65536, 3456], P(('node', 'table')), may hold values from -0.1796875 to 0.1796875
Outputs:
- cross_out: bfloat16 [65536, 3456], P(('node', 'table'))
- emb_grad: float32 [131072, 128], P(('node', 'table'))
The draws below stay inside these ranges and needn't reach their ends.
Inputs may be any that keep to these rules, and one draw needn't show every extreme that they name: For each node index n and table index t, take the tiles j with j // 16 == n on the 4 devices of table index t: no tile_table value occurs more than 3 times among them, and the tiles with one value carry at most 2 distinct tile_slot values. Both bounds are reached in every such set.
All inputs are finite; a program needn't handle non-finite values.
Results may differ from the reference program's by a relative error of at most 0.0057.
Values may be sent and summed in bfloat16 or wider, within the bound.
A program may use at most 128 MiB of HBM per device.

```python
import jax
import jax.numpy as jnp
from jax import lax

EMB = 128
FEATURES = 26
RANK = 512
BLOCK = 128
SAMP_DEV = 256
ROW_BLOCKS = 4
TILE_LIST = 1
TILES = 64
SAMPLE_BLOCKS = 2
BAG_BLOCKS = 52
CROSS = 3456
SAMPLES = 65536
ROWS = 131072
N_NODE = 4
N_TABLE = 64
DEVICES = 256


def routing(key):
    stream = jax.random.split(jax.random.fold_in(key, 11), 4)
    groups = N_NODE * N_TABLE
    length = TILE_LIST * N_TABLE
    heavy_count = jax.random.randint(stream[0], (groups, 1), 1, N_TABLE // 4 + 1)
    position = jax.vmap(lambda subkey: jax.random.permutation(subkey, length))(jax.random.split(stream[1], groups))
    shuffle = jax.vmap(lambda subkey: jax.random.permutation(subkey, N_TABLE))(jax.random.split(stream[2], groups))
    heavy_size = 3 * TILE_LIST
    heavy_edge = heavy_size * heavy_count
    leading = position < heavy_edge
    member = jnp.where(leading, position // heavy_size, heavy_count + (position - heavy_edge) // TILE_LIST)
    within = jnp.where(leading, position % heavy_size % (2 * TILE_LIST), (position - heavy_edge) % TILE_LIST)
    table_ids = jnp.take_along_axis(shuffle, member, axis=1)
    base_slot = jax.random.randint(stream[3], (groups, N_TABLE), 0, BAG_BLOCKS)
    slot_ids = (jnp.take_along_axis(base_slot, member, axis=1) + within) % BAG_BLOCKS
    layout = (N_NODE, N_TABLE, N_NODE, length // N_NODE)
    table_out = table_ids.reshape(layout).transpose(2, 1, 0, 3).reshape(-1).astype(jnp.int32)
    slot_out = slot_ids.reshape(layout).transpose(2, 1, 0, 3).reshape(-1).astype(jnp.int32)
    return (table_out, slot_out)


def draw_tile_table(key, part):
    return routing(key)[0]


def draw_tile_slot(key, part):
    return routing(key)[1]


def touch_ends(drawn, own_key, least, top_value):
    longest = drawn.shape.index(max(drawn.shape))
    spots = []
    for shift in (0, 1):
        where = [jax.random.randint(jax.random.fold_in(own_key, axis), (), 0, length) for axis, length in enumerate(drawn.shape)]
        where[longest] = (where[longest] + shift) % drawn.shape[longest]
        spots.append(tuple(where))
    return drawn.at[spots[0]].set(least).at[spots[1]].set(top_value)


def levels(stream_key, extent, cuts, smallest, top_value):
    loudness = 1.0
    for dim, blocks in cuts:
        draws = jax.random.uniform(jax.random.fold_in(jax.random.fold_in(stream_key, 6), dim), (blocks,), jnp.float32, smallest / len(cuts), top_value / len(cuts))
        loudness = loudness * jnp.repeat(jnp.exp(draws), extent[dim] // blocks).reshape((-1,) + (1,) * (len(extent) - 1 - dim))
    return loudness


def centred(rng, shape, spread, limit, cuts=(), held_as=jnp.bfloat16):
    gain = levels(rng, shape, cuts, -0.22, 0.18) if cuts else 1.0
    result = jax.random.normal(rng, shape, jnp.float32) * spread * gain
    return jnp.minimum(jnp.maximum(result, -limit), limit).astype(held_as)


def setup_inputs(seed: int = 0) -> dict:
    arg_keys = jax.random.split(jax.random.key(seed), 11)
    return {
        "emb_rows": centred(arg_keys[0], (ROWS, EMB), 0.04, 0.23925781, ((0, 256),)),
        "tile_mult": touch_ends(jax.random.randint(arg_keys[1], (DEVICES * TILES, BLOCK, BLOCK), 0, 4), jax.random.fold_in(arg_keys[1], 1), 0, 3).astype(jnp.int32),
        "tile_rows": touch_ends(jax.random.randint(arg_keys[2], (DEVICES * TILES,), 0, ROW_BLOCKS), jax.random.fold_in(arg_keys[2], 1), 0, ROW_BLOCKS - 1).astype(jnp.int32),
        "tile_table": draw_tile_table(jax.random.fold_in(arg_keys[10], 71), 0),
        "tile_slot": draw_tile_slot(jax.random.fold_in(arg_keys[10], 71), 0),
        "dense": centred(arg_keys[5], (SAMPLES, EMB), 1.0, 6.0, ((0, 256),)),
        "cross_v": centred(arg_keys[6], (CROSS, RANK), CROSS ** -0.5, 0.109375, ((0, 4),)),
        "cross_u": centred(arg_keys[7], (RANK, CROSS), RANK ** -0.5, 0.25, ((0, 4),)),
        "cross_bias": centred(arg_keys[8], (CROSS,), 0.5, 3.0, (), jnp.float32),
        "cotangent": centred(arg_keys[9], (SAMPLES, CROSS), 0.03, 0.1796875, ((0, 256),)),
    }


def cross_owner(first_layer, cross_v, cross_u, cross_bias, cotangent):
    hidden = jnp.dot(first_layer, cross_v, preferred_element_type=jnp.float32).astype(jnp.bfloat16)
    cross_scale = jnp.dot(hidden, cross_u, preferred_element_type=jnp.float32) + cross_bias
    layer_input = first_layer.astype(jnp.float32)
    cross_out = (layer_input * (cross_scale + 1.0)).astype(jnp.bfloat16)
    upstream = cotangent.astype(jnp.float32)
    dscale = (upstream * layer_input).astype(jnp.bfloat16)
    dhidden = jnp.dot(dscale, cross_u.T, preferred_element_type=jnp.float32).astype(jnp.bfloat16)
    dlayer = upstream * (cross_scale + 1.0) + jnp.dot(dhidden, cross_v.T, preferred_element_type=jnp.float32)
    return cross_out, dlayer[:, EMB:].astype(jnp.bfloat16)


def reference(emb_rows, tile_mult, tile_rows, tile_table, tile_slot, dense, cross_v, cross_u, cross_bias, cotangent):
    devices = N_NODE * N_TABLE
    quarter = TILES // N_NODE
    row_blocks = emb_rows.reshape(devices, ROW_BLOCKS, BLOCK, EMB)
    tile_weights = tile_mult.reshape(devices, TILES, BLOCK, BLOCK)
    dest_node = jnp.arange(TILES, dtype=jnp.int32) // quarter
    owner_ids = dest_node[None, :] * N_TABLE + tile_table.reshape(devices, TILES).astype(jnp.int32)
    bag_index = (owner_ids * BAG_BLOCKS + tile_slot.reshape(devices, TILES).astype(jnp.int32)).astype(jnp.int32)
    rows_local = tile_rows.reshape(devices, TILES).astype(jnp.int32)

    def gather_pool(running, inputs):
        blocks, weights, local_rows, target = inputs
        picked = jnp.take(blocks, local_rows, axis=0).astype(jnp.float32)
        partial_rows = jnp.einsum("kbr,kre->kbe", weights.astype(jnp.float32), picked, precision=lax.Precision.HIGHEST)
        return running.at[target].add(partial_rows), None

    pooled = lax.scan(gather_pool, jnp.zeros((devices * BAG_BLOCKS, BLOCK, EMB), jnp.float32), (row_blocks, tile_weights, rows_local, bag_index))[0]
    embedded = pooled.reshape(devices, FEATURES, SAMPLE_BLOCKS, BLOCK, EMB).transpose(0, 2, 3, 1, 4)
    embedded = embedded.reshape(devices, SAMP_DEV, FEATURES * EMB).astype(jnp.bfloat16)
    first_layer = jnp.concatenate([dense.reshape(devices, SAMP_DEV, EMB), embedded], axis=2)
    cross_out, bag_grad = lax.map(lambda packed: cross_owner(packed[0], cross_v, cross_u, cross_bias, packed[1]), (first_layer, cotangent.reshape(devices, SAMP_DEV, CROSS)))
    bag_grad = bag_grad.reshape(devices, SAMPLE_BLOCKS, BLOCK, FEATURES, EMB).transpose(0, 3, 1, 2, 4)
    bag_grad = bag_grad.reshape(devices * BAG_BLOCKS, BLOCK, EMB)

    def row_grads(inputs):
        weights, local_rows, target = inputs
        back_rows = jnp.take(bag_grad, target, axis=0).astype(jnp.float32)
        tile_grads = jnp.einsum("kbr,kbe->kre", weights.astype(jnp.float32), back_rows, precision=lax.Precision.HIGHEST)
        return jnp.zeros((ROW_BLOCKS, BLOCK, EMB), jnp.float32).at[local_rows].add(tile_grads)

    emb_grad = lax.map(row_grads, (tile_weights, rows_local, bag_index)).reshape(devices * ROW_BLOCKS * BLOCK, EMB)
    return cross_out.reshape(devices * SAMP_DEV, CROSS), emb_grad
```

```python
import jax
import jax.numpy as jnp
from jax import lax
from jax.sharding import PartitionSpec as P

FEATURES = 26
DEPTH = 2
SAMPLE_BLOCKS = 2
BAG_BLOCKS = 52


def owner_work(arrived, arrived_slot, dense, cross_v, cross_u, cross_bias, cotangent):
    block_size = arrived.shape[-2]
    emb_width = arrived.shape[-1]
    flat_arrived = arrived.reshape(-1, block_size * emb_width)
    flat_slot = arrived_slot.reshape(-1)
    selector = flat_slot[None, :] == jnp.arange(BAG_BLOCKS, dtype=jnp.int32)[:, None]
    pooled = jnp.dot(
        selector.astype(jnp.bfloat16), flat_arrived, preferred_element_type=jnp.float32
    )
    embedded = pooled.reshape(FEATURES, SAMPLE_BLOCKS, block_size, emb_width).transpose(1, 2, 0, 3)
    embedded = embedded.reshape(-1, FEATURES * emb_width).astype(jnp.bfloat16)
    first_layer = jnp.concatenate([dense, embedded], axis=1)
    hidden = jnp.dot(first_layer, cross_v, preferred_element_type=jnp.float32).astype(jnp.bfloat16)
    cross_scale = jnp.dot(hidden, cross_u, preferred_element_type=jnp.float32) + cross_bias
    layer_input = first_layer.astype(jnp.float32)
    cross_out = (layer_input * (cross_scale + 1.0)).astype(jnp.bfloat16)
    upstream = cotangent.astype(jnp.float32)
    dscale = (upstream * layer_input).astype(jnp.bfloat16)
    dhidden = lax.dot_general(
        dscale, cross_u, (((1,), (1,)), ((), ())), preferred_element_type=jnp.float32
    ).astype(jnp.bfloat16)
    dlayer = upstream * (cross_scale + 1.0) + lax.dot_general(
        dhidden, cross_v, (((1,), (1,)), ((), ())), preferred_element_type=jnp.float32
    )
    bag_grad = (
        dlayer[:, emb_width:]
        .astype(jnp.bfloat16)
        .reshape(SAMPLE_BLOCKS, block_size, FEATURES, emb_width)
    )
    bag_grad = bag_grad.transpose(2, 0, 1, 3).reshape(BAG_BLOCKS, block_size * emb_width)
    returning = lax.dot_general(
        selector.astype(jnp.bfloat16), bag_grad, (((0,), (0,)), ((), ())),
        preferred_element_type=jnp.float32,
    ).astype(jnp.bfloat16)
    return cross_out, returning.reshape(arrived.shape)


def body(
    emb_rows,
    tile_mult,
    tile_rows,
    tile_table,
    tile_slot,
    dense,
    cross_v,
    cross_u,
    cross_bias,
    cotangent,
):
    tables = lax.axis_size("table")
    nodes = lax.axis_size("node")
    tile_count = tile_mult.shape[0]
    block_size = tile_mult.shape[1]
    emb_width = emb_rows.shape[1]
    local_blocks = emb_rows.shape[0] // block_size
    row_blocks = emb_rows.reshape(-1, block_size, emb_width)
    mult_bf = tile_mult.astype(jnp.bfloat16)

    meta = jnp.stack([tile_table, tile_slot, tile_rows], axis=1)
    moved_meta = lax.all_to_all(meta, "node", split_axis=0, concat_axis=0, tiled=True)
    moved_mult = lax.all_to_all(mult_bf, "node", split_axis=0, concat_axis=0, tiled=True)
    peer_rows = lax.all_gather(row_blocks, "node", axis=0, tiled=True)
    full_v = lax.all_gather(cross_v, "node", axis=0, tiled=True)
    full_u = lax.all_gather(cross_u, "node", axis=0, tiled=True)

    moved_table = moved_meta[:, 0]
    moved_slot = moved_meta[:, 1]
    sequence = jnp.arange(tile_count, dtype=jnp.int32)
    source = sequence // (tile_count // nodes)
    moved_rows = source * local_blocks + moved_meta[:, 2]
    picked = jnp.take(peer_rows, moved_rows, axis=0)
    products = jnp.einsum(
        "kbr,kre->kbe", moved_mult, picked, preferred_element_type=jnp.float32
    ).reshape(tile_count, -1)

    same_table = moved_table[:, None] == moved_table[None, :]
    first = jnp.min(jnp.where(same_table, sequence[None, :], tile_count), axis=1)
    first_slot = jnp.take(moved_slot, first)
    entry = moved_table * DEPTH + (moved_slot != first_slot).astype(jnp.int32)
    entries = tables * DEPTH
    chosen = entry[None, :] == jnp.arange(entries, dtype=jnp.int32)[:, None]
    send_rows = jnp.dot(
        chosen.astype(jnp.float32), products, precision=lax.Precision.HIGHEST,
        preferred_element_type=jnp.float32,
    ).astype(jnp.bfloat16)
    send_slot = jnp.max(jnp.where(chosen, moved_slot[None, :], -1), axis=1)

    arrived = lax.all_to_all(
        send_rows.reshape(tables, DEPTH, block_size, emb_width),
        "table", split_axis=0, concat_axis=0, tiled=True,
    )
    arrived_slot = lax.all_to_all(
        send_slot.reshape(tables, DEPTH), "table", split_axis=0, concat_axis=0, tiled=True
    )
    cross_out, returning = owner_work(
        arrived, arrived_slot, dense, full_v, full_u, cross_bias, cotangent
    )
    came_back = lax.all_to_all(returning, "table", split_axis=0, concat_axis=0, tiled=True)
    tile_grad = lax.dot_general(
        chosen.astype(jnp.bfloat16), came_back.reshape(entries, -1), (((0,), (0,)), ((), ())),
        preferred_element_type=jnp.float32,
    ).astype(jnp.bfloat16)
    tile_grad = lax.all_to_all(
        tile_grad.reshape(tile_count, block_size, emb_width),
        "node", split_axis=0, concat_axis=0, tiled=True,
    )
    tile_grads = jnp.einsum(
        "kbr,kbe->kre", mult_bf, tile_grad, preferred_element_type=jnp.float32
    )
    owner_rows = (
        tile_rows[None, :] == jnp.arange(local_blocks, dtype=jnp.int32)[:, None]
    ).astype(jnp.float32)
    emb_grad = jnp.dot(
        owner_rows,
        tile_grads.reshape(tile_count, -1),
        precision=lax.Precision.HIGHEST,
        preferred_element_type=jnp.float32,
    )
    return (cross_out, emb_grad.reshape(-1, emb_width))


def solution(mesh):
    in_specs = (
        P(("node", "table"), None),
        P(("node", "table"), None, None),
        P(("node", "table")),
        P(("node", "table")),
        P(("node", "table")),
        P(("node", "table"), None),
        P("node", None),
        P("node", None),
        P(),
        P(("node", "table"), None),
    )
    out_specs = (P(("node", "table"), None), P(("node", "table"), None))
    return jax.shard_map(body, mesh=mesh, in_specs=in_specs, out_specs=out_specs, check_vma=False)
```

```python
import jax
import jax.numpy as jnp
from jax import lax
from jax.sharding import PartitionSpec as P

FEATURES = 26
DEPTH = 2
SAMPLE_BLOCKS = 2
BAG_BLOCKS = 52


def owner_work(arrived, arrived_slot, dense, cross_v, cross_u, cross_bias, cotangent):
    block_size = arrived.shape[-2]
    emb_width = arrived.shape[-1]
    flat_arrived = arrived.reshape(-1, block_size * emb_width)
    flat_slot = arrived_slot.reshape(-1)
    selector = flat_slot[None, :] == jnp.arange(BAG_BLOCKS, dtype=jnp.int32)[:, None]
    pooled = jnp.dot(
        selector.astype(jnp.bfloat16), flat_arrived, preferred_element_type=jnp.float32
    )
    embedded = pooled.reshape(FEATURES, SAMPLE_BLOCKS, block_size, emb_width).transpose(1, 2, 0, 3)
    embedded = embedded.reshape(-1, FEATURES * emb_width).astype(jnp.bfloat16)
    first_layer = jnp.concatenate([dense, embedded], axis=1)
    hidden = jnp.dot(first_layer, cross_v, preferred_element_type=jnp.float32).astype(jnp.bfloat16)
    cross_scale = jnp.dot(hidden, cross_u, preferred_element_type=jnp.float32) + cross_bias
    layer_input = first_layer.astype(jnp.float32)
    cross_out = (layer_input * (cross_scale + 1.0)).astype(jnp.bfloat16)
    upstream = cotangent.astype(jnp.float32)
    dscale = (upstream * layer_input).astype(jnp.bfloat16)
    dhidden = lax.dot_general(
        dscale, cross_u, (((1,), (1,)), ((), ())), preferred_element_type=jnp.float32
    ).astype(jnp.bfloat16)
    dlayer = upstream * (cross_scale + 1.0) + lax.dot_general(
        dhidden, cross_v, (((1,), (1,)), ((), ())), preferred_element_type=jnp.float32
    )
    bag_grad = (
        dlayer[:, emb_width:]
        .astype(jnp.bfloat16)
        .reshape(SAMPLE_BLOCKS, block_size, FEATURES, emb_width)
    )
    bag_grad = bag_grad.transpose(2, 0, 1, 3).reshape(BAG_BLOCKS, block_size * emb_width)
    returning = lax.dot_general(
        selector.astype(jnp.bfloat16), bag_grad, (((0,), (0,)), ((), ())),
        preferred_element_type=jnp.float32,
    ).astype(jnp.bfloat16)
    return cross_out, returning.reshape(arrived.shape)


def body(
    emb_rows,
    tile_mult,
    tile_rows,
    tile_table,
    tile_slot,
    dense,
    cross_v,
    cross_u,
    cross_bias,
    cotangent,
):
    tables = lax.axis_size("table")
    nodes = lax.axis_size("node")
    tile_count = tile_mult.shape[0]
    block_size = tile_mult.shape[1]
    emb_width = emb_rows.shape[1]
    local_blocks = emb_rows.shape[0] // block_size
    row_blocks = emb_rows.reshape(-1, block_size, emb_width)
    mult_bf = tile_mult.astype(jnp.bfloat16)

    per_node = tile_count // nodes
    meta = jnp.stack([tile_table, tile_slot, tile_rows], axis=1).astype(jnp.bfloat16)
    meta_block = jnp.zeros((nodes, block_size, emb_width), jnp.bfloat16)
    meta_block = meta_block.at[:, :per_node, :3].set(meta.reshape(nodes, per_node, 3))
    outgoing = jnp.concatenate(
        [
            mult_bf.reshape(nodes, per_node, block_size, block_size),
            jnp.broadcast_to(row_blocks[None], (nodes, local_blocks, block_size, emb_width)),
            meta_block[:, None],
        ],
        axis=1,
    )
    incoming = lax.all_to_all(outgoing, "node", split_axis=0, concat_axis=0, tiled=True)
    full_v = lax.all_gather(cross_v, "node", axis=0, tiled=True)
    full_u = lax.all_gather(cross_u, "node", axis=0, tiled=True)
    moved_mult = incoming[:, :per_node].reshape(tile_count, block_size, block_size)
    peer_rows = incoming[:, per_node:per_node + local_blocks].reshape(-1, block_size, emb_width)
    moved_meta = incoming[:, -1, :per_node, :3].reshape(tile_count, 3).astype(jnp.int32)

    moved_table = moved_meta[:, 0]
    moved_slot = moved_meta[:, 1]
    sequence = jnp.arange(tile_count, dtype=jnp.int32)
    source = sequence // per_node
    moved_rows = source * local_blocks + moved_meta[:, 2]
    picked = jnp.take(peer_rows, moved_rows, axis=0)
    products = jnp.einsum(
        "kbr,kre->kbe", moved_mult, picked, preferred_element_type=jnp.float32
    ).reshape(tile_count, -1)

    same_table = moved_table[:, None] == moved_table[None, :]
    first = jnp.min(jnp.where(same_table, sequence[None, :], tile_count), axis=1)
    first_slot = jnp.take(moved_slot, first)
    entry = moved_table * DEPTH + (moved_slot != first_slot).astype(jnp.int32)
    entries = tables * DEPTH
    chosen = entry[None, :] == jnp.arange(entries, dtype=jnp.int32)[:, None]
    send_rows = jnp.dot(
        chosen.astype(jnp.float32), products, precision=lax.Precision.HIGHEST,
        preferred_element_type=jnp.float32,
    ).astype(jnp.bfloat16)
    send_slot = jnp.max(jnp.where(chosen, moved_slot[None, :], -1), axis=1)

    arrived = lax.all_to_all(
        send_rows.reshape(tables, DEPTH, block_size, emb_width),
        "table", split_axis=0, concat_axis=0, tiled=True,
    )
    arrived_slot = lax.all_to_all(
        send_slot.reshape(tables, DEPTH), "table", split_axis=0, concat_axis=0, tiled=True
    )
    cross_out, returning = owner_work(
        arrived, arrived_slot, dense, full_v, full_u, cross_bias, cotangent
    )
    came_back = lax.all_to_all(returning, "table", split_axis=0, concat_axis=0, tiled=True)
    tile_grad = lax.dot_general(
        chosen.astype(jnp.bfloat16), came_back.reshape(entries, -1), (((0,), (0,)), ((), ())),
        preferred_element_type=jnp.float32,
    ).astype(jnp.bfloat16)
    tile_grad = lax.all_to_all(
        tile_grad.reshape(tile_count, block_size, emb_width),
        "node", split_axis=0, concat_axis=0, tiled=True,
    )
    tile_grads = jnp.einsum(
        "kbr,kbe->kre", mult_bf, tile_grad, preferred_element_type=jnp.float32
    )
    owner_rows = (
        tile_rows[None, :] == jnp.arange(local_blocks, dtype=jnp.int32)[:, None]
    ).astype(jnp.float32)
    emb_grad = jnp.dot(
        owner_rows,
        tile_grads.reshape(tile_count, -1),
        precision=lax.Precision.HIGHEST,
        preferred_element_type=jnp.float32,
    )
    return (cross_out, emb_grad.reshape(-1, emb_width))


def solution(mesh):
    in_specs = (
        P(("node", "table"), None),
        P(("node", "table"), None, None),
        P(("node", "table")),
        P(("node", "table")),
        P(("node", "table")),
        P(("node", "table"), None),
        P("node", None),
        P("node", None),
        P(),
        P(("node", "table"), None),
    )
    out_specs = (P(("node", "table"), None), P(("node", "table"), None))
    return jax.shard_map(body, mesh=mesh, in_specs=in_specs, out_specs=out_specs, check_vma=False)
```

```python
import jax
import jax.numpy as jnp
from jax import lax
from jax.experimental import pallas as pl
from jax.experimental.pallas import tpu as pltpu
from jax.sharding import PartitionSpec as P

FEATURES = 26
DEPTH = 2
SAMPLE_BLOCKS = 2
BAG_BLOCKS = 52


def cross_kernel(
    slot_ref, arrived_ref, dense_ref, v_ref, u_ref, bias_ref, cot_ref,
    out_ref, ret_ref, pooled_ref, layer_ref, dscale_ref, dlayer_ref, bag_ref,
):
    entries, block_size, emb_width = arrived_ref.shape
    bags = pooled_ref.shape[0]
    chunks = layer_ref.shape[1] // emb_width
    f32, bf16 = jnp.float32, jnp.bfloat16

    pooled_ref[...] = jnp.zeros_like(pooled_ref)

    def pool(i, carry):
        slot = slot_ref[i]

        @pl.when(slot >= 0)
        def _():
            pooled_ref[slot] += arrived_ref[i].astype(f32)

        return carry

    lax.fori_loop(0, entries, pool, 0)
    layer_ref[:, 0:emb_width] = dense_ref[...]
    for bag in range(bags):
        feature, half = divmod(bag, SAMPLE_BLOCKS)
        layer_ref[
            half * block_size:(half + 1) * block_size,
            (feature + 1) * emb_width:(feature + 2) * emb_width,
        ] = pooled_ref[bag].astype(bf16)

    hidden = jnp.dot(layer_ref[...], v_ref[...], preferred_element_type=f32).astype(bf16)

    def forward(c, carry):
        cols = pl.ds(pl.multiple_of(c * emb_width, emb_width), emb_width)
        scale = jnp.dot(hidden, u_ref[:, cols], preferred_element_type=f32) + bias_ref[:, cols]
        layer_input = layer_ref[:, cols].astype(f32)
        upstream = cot_ref[:, cols].astype(f32)
        out_ref[:, cols] = (layer_input * (scale + 1.0)).astype(bf16)
        dscale_ref[:, cols] = (upstream * layer_input).astype(bf16)
        dlayer_ref[:, cols] = upstream * (scale + 1.0)
        return carry

    lax.fori_loop(0, chunks, forward, 0)
    dhidden = lax.dot_general(
        dscale_ref[...], u_ref[...], (((1,), (1,)), ((), ())), preferred_element_type=f32
    ).astype(bf16)

    def backward(feature, carry):
        start = pl.multiple_of((feature + 1) * emb_width, emb_width)
        cols = pl.ds(start, emb_width)
        dlayer = dlayer_ref[:, cols] + lax.dot_general(
            dhidden, v_ref[cols, :], (((1,), (1,)), ((), ())), preferred_element_type=f32
        )
        grad = dlayer.astype(bf16)
        for half in range(SAMPLE_BLOCKS):
            bag_ref[feature * SAMPLE_BLOCKS + half] = grad[half * block_size:(half + 1) * block_size]
        return carry

    lax.fori_loop(0, chunks - 1, backward, 0)

    def gather_back(i, carry):
        slot = slot_ref[i]
        picked = bag_ref[jnp.maximum(slot, 0)]
        ret_ref[i] = jnp.where(slot >= 0, picked, jnp.zeros_like(picked))
        return carry

    lax.fori_loop(0, entries, gather_back, 0)


def owner_work(arrived, arrived_slot, dense, cross_v, cross_u, cross_bias, cotangent):
    block_size = arrived.shape[-2]
    emb_width = arrived.shape[-1]
    entries = arrived.shape[0] * arrived.shape[1]
    samples, width = cotangent.shape
    rank = cross_v.shape[1]
    vmem = pl.BlockSpec(memory_space=pltpu.VMEM)
    flops = 8 * samples * width * rank
    nbytes = 2 * (2 * entries * block_size * emb_width + 2 * width * rank + 2 * samples * width)
    cross_out, returning = pl.pallas_call(
        cross_kernel,
        out_shape=(
            jax.ShapeDtypeStruct((samples, width), jnp.bfloat16),
            jax.ShapeDtypeStruct((entries, block_size, emb_width), jnp.bfloat16),
        ),
        in_specs=[pl.BlockSpec(memory_space=pltpu.SMEM)] + [vmem] * 6,
        out_specs=(vmem, vmem),
        scratch_shapes=[
            pltpu.VMEM((BAG_BLOCKS, block_size, emb_width), jnp.float32),
            pltpu.VMEM((samples, width), jnp.bfloat16),
            pltpu.VMEM((samples, width), jnp.bfloat16),
            pltpu.VMEM((samples, width), jnp.float32),
            pltpu.VMEM((BAG_BLOCKS, block_size, emb_width), jnp.bfloat16),
        ],
        compiler_params=pltpu.CompilerParams(vmem_limit_bytes=64 * 1024 * 1024),
        cost_estimate=pl.CostEstimate(flops=flops, bytes_accessed=nbytes, transcendentals=0),
    )(
        arrived_slot.reshape(-1),
        arrived.reshape(entries, block_size, emb_width),
        dense,
        cross_v,
        cross_u,
        cross_bias.reshape(1, -1),
        cotangent,
    )
    return cross_out, returning.reshape(arrived.shape)


def body(
    emb_rows,
    tile_mult,
    tile_rows,
    tile_table,
    tile_slot,
    dense,
    cross_v,
    cross_u,
    cross_bias,
    cotangent,
):
    tables = lax.axis_size("table")
    nodes = lax.axis_size("node")
    tile_count = tile_mult.shape[0]
    block_size = tile_mult.shape[1]
    emb_width = emb_rows.shape[1]
    local_blocks = emb_rows.shape[0] // block_size
    row_blocks = emb_rows.reshape(-1, block_size, emb_width)
    mult_bf = tile_mult.astype(jnp.bfloat16)

    per_node = tile_count // nodes
    meta = jnp.stack([tile_table, tile_slot, tile_rows], axis=1).astype(jnp.bfloat16)
    meta_block = jnp.zeros((nodes, block_size, emb_width), jnp.bfloat16)
    meta_block = meta_block.at[:, :per_node, :3].set(meta.reshape(nodes, per_node, 3))
    outgoing = jnp.concatenate(
        [
            mult_bf.reshape(nodes, per_node, block_size, block_size),
            jnp.broadcast_to(row_blocks[None], (nodes, local_blocks, block_size, emb_width)),
            meta_block[:, None],
        ],
        axis=1,
    )
    incoming = lax.all_to_all(outgoing, "node", split_axis=0, concat_axis=0, tiled=True)
    full_v = lax.all_gather(cross_v, "node", axis=0, tiled=True)
    full_u = lax.all_gather(cross_u, "node", axis=0, tiled=True)
    moved_mult = incoming[:, :per_node].reshape(tile_count, block_size, block_size)
    peer_rows = incoming[:, per_node:per_node + local_blocks].reshape(-1, block_size, emb_width)
    moved_meta = incoming[:, -1, :per_node, :3].reshape(tile_count, 3).astype(jnp.int32)

    moved_table = moved_meta[:, 0]
    moved_slot = moved_meta[:, 1]
    sequence = jnp.arange(tile_count, dtype=jnp.int32)
    source = sequence // per_node
    moved_rows = source * local_blocks + moved_meta[:, 2]
    picked = jnp.take(peer_rows, moved_rows, axis=0)
    products = jnp.einsum(
        "kbr,kre->kbe", moved_mult, picked, preferred_element_type=jnp.float32
    ).reshape(tile_count, -1)

    same_table = moved_table[:, None] == moved_table[None, :]
    first = jnp.min(jnp.where(same_table, sequence[None, :], tile_count), axis=1)
    first_slot = jnp.take(moved_slot, first)
    entry = moved_table * DEPTH + (moved_slot != first_slot).astype(jnp.int32)
    entries = tables * DEPTH
    chosen = entry[None, :] == jnp.arange(entries, dtype=jnp.int32)[:, None]
    send_rows = jnp.dot(
        chosen.astype(jnp.float32), products, precision=lax.Precision.HIGHEST,
        preferred_element_type=jnp.float32,
    ).astype(jnp.bfloat16)
    send_slot = jnp.max(jnp.where(chosen, moved_slot[None, :], -1), axis=1)

    arrived = lax.all_to_all(
        send_rows.reshape(tables, DEPTH, block_size, emb_width),
        "table", split_axis=0, concat_axis=0, tiled=True,
    )
    arrived_slot = lax.all_to_all(
        send_slot.reshape(tables, DEPTH), "table", split_axis=0, concat_axis=0, tiled=True
    )
    cross_out, returning = owner_work(
        arrived, arrived_slot, dense, full_v, full_u, cross_bias, cotangent
    )
    came_back = lax.all_to_all(returning, "table", split_axis=0, concat_axis=0, tiled=True)
    tile_grad = lax.dot_general(
        chosen.astype(jnp.bfloat16), came_back.reshape(entries, -1), (((0,), (0,)), ((), ())),
        preferred_element_type=jnp.float32,
    ).astype(jnp.bfloat16)
    tile_grad = lax.all_to_all(
        tile_grad.reshape(tile_count, block_size, emb_width),
        "node", split_axis=0, concat_axis=0, tiled=True,
    )
    tile_grads = jnp.einsum(
        "kbr,kbe->kre", mult_bf, tile_grad, preferred_element_type=jnp.float32
    )
    owner_rows = (
        tile_rows[None, :] == jnp.arange(local_blocks, dtype=jnp.int32)[:, None]
    ).astype(jnp.float32)
    emb_grad = jnp.dot(
        owner_rows,
        tile_grads.reshape(tile_count, -1),
        precision=lax.Precision.HIGHEST,
        preferred_element_type=jnp.float32,
    )
    return (cross_out, emb_grad.reshape(-1, emb_width))


def solution(mesh):
    in_specs = (
        P(("node", "table"), None),
        P(("node", "table"), None, None),
        P(("node", "table")),
        P(("node", "table")),
        P(("node", "table")),
        P(("node", "table"), None),
        P("node", None),
        P("node", None),
        P(),
        P(("node", "table"), None),
    )
    out_specs = (P(("node", "table"), None), P(("node", "table"), None))
    return jax.shard_map(body, mesh=mesh, in_specs=in_specs, out_specs=out_specs, check_vma=False)
```

```python
import jax
import jax.numpy as jnp
from jax import lax
from jax.experimental import pallas as pl
from jax.experimental.pallas import tpu as pltpu
from jax.sharding import PartitionSpec as P

FEATURES = 26
DEPTH = 2
SLOT_ROWS = 8
SAMPLE_BLOCKS = 2
BAG_BLOCKS = 52


def cross_kernel(
    slot_ref, arrived_ref, dense_ref, v_ref, u_ref, bias_ref, cot_ref,
    out_ref, ret_ref, pooled_ref, layer_ref, dscale_ref, dlayer_ref, bag_ref,
):
    entries, block_size, emb_width = ret_ref.shape
    bags = pooled_ref.shape[0]
    chunks = layer_ref.shape[1] // emb_width
    f32, bf16 = jnp.float32, jnp.bfloat16

    pooled_ref[...] = jnp.zeros_like(pooled_ref)

    def pool(i, carry):
        slot = slot_ref[i]

        @pl.when(slot >= 0)
        def _():
            rows = pl.ds(pl.multiple_of((i % DEPTH) * block_size, block_size), block_size)
            pooled_ref[slot] += arrived_ref[i // DEPTH, rows, :].astype(f32)

        return carry

    lax.fori_loop(0, entries, pool, 0)
    layer_ref[:, 0:emb_width] = dense_ref[...]
    for bag in range(bags):
        feature, half = divmod(bag, SAMPLE_BLOCKS)
        layer_ref[
            half * block_size:(half + 1) * block_size,
            (feature + 1) * emb_width:(feature + 2) * emb_width,
        ] = pooled_ref[bag].astype(bf16)

    hidden = jnp.dot(layer_ref[...], v_ref[...], preferred_element_type=f32).astype(bf16)

    def forward(c, carry):
        cols = pl.ds(pl.multiple_of(c * emb_width, emb_width), emb_width)
        scale = jnp.dot(hidden, u_ref[:, cols], preferred_element_type=f32) + bias_ref[:, cols]
        layer_input = layer_ref[:, cols].astype(f32)
        upstream = cot_ref[:, cols].astype(f32)
        out_ref[:, cols] = (layer_input * (scale + 1.0)).astype(bf16)
        dscale_ref[:, cols] = (upstream * layer_input).astype(bf16)
        dlayer_ref[:, cols] = upstream * (scale + 1.0)
        return carry

    lax.fori_loop(0, chunks, forward, 0)
    dhidden = lax.dot_general(
        dscale_ref[...], u_ref[...], (((1,), (1,)), ((), ())), preferred_element_type=f32
    ).astype(bf16)

    def backward(feature, carry):
        start = pl.multiple_of((feature + 1) * emb_width, emb_width)
        cols = pl.ds(start, emb_width)
        dlayer = dlayer_ref[:, cols] + lax.dot_general(
            dhidden, v_ref[cols, :], (((1,), (1,)), ((), ())), preferred_element_type=f32
        )
        grad = dlayer.astype(bf16)
        for half in range(SAMPLE_BLOCKS):
            bag_ref[feature * SAMPLE_BLOCKS + half] = grad[half * block_size:(half + 1) * block_size]
        return carry

    lax.fori_loop(0, chunks - 1, backward, 0)

    def gather_back(i, carry):
        slot = slot_ref[i]
        picked = bag_ref[jnp.maximum(slot, 0)]
        ret_ref[i] = jnp.where(slot >= 0, picked, jnp.zeros_like(picked))
        return carry

    lax.fori_loop(0, entries, gather_back, 0)


def owner_work(arrived, arrived_slot, dense, cross_v, cross_u, cross_bias, cotangent):
    emb_width = arrived.shape[-1]
    block_size = emb_width
    entries = arrived.shape[0] * DEPTH
    samples, width = cotangent.shape
    rank = cross_v.shape[1]
    vmem = pl.BlockSpec(memory_space=pltpu.VMEM)
    flops = 8 * samples * width * rank
    nbytes = 2 * (2 * entries * block_size * emb_width + 2 * width * rank + 2 * samples * width)
    cross_out, returning = pl.pallas_call(
        cross_kernel,
        out_shape=(
            jax.ShapeDtypeStruct((samples, width), jnp.bfloat16),
            jax.ShapeDtypeStruct((entries, block_size, emb_width), jnp.bfloat16),
        ),
        in_specs=[pl.BlockSpec(memory_space=pltpu.SMEM)] + [vmem] * 6,
        out_specs=(vmem, vmem),
        scratch_shapes=[
            pltpu.VMEM((BAG_BLOCKS, block_size, emb_width), jnp.float32),
            pltpu.VMEM((samples, width), jnp.bfloat16),
            pltpu.VMEM((samples, width), jnp.bfloat16),
            pltpu.VMEM((samples, width), jnp.float32),
            pltpu.VMEM((BAG_BLOCKS, block_size, emb_width), jnp.bfloat16),
        ],
        compiler_params=pltpu.CompilerParams(vmem_limit_bytes=64 * 1024 * 1024),
        cost_estimate=pl.CostEstimate(flops=flops, bytes_accessed=nbytes, transcendentals=0),
    )(
        arrived_slot.reshape(-1),
        arrived,
        dense,
        cross_v,
        cross_u,
        cross_bias.reshape(1, -1),
        cotangent,
    )
    return cross_out, returning.reshape(-1, DEPTH, block_size, emb_width)


def body(
    emb_rows,
    tile_mult,
    tile_rows,
    tile_table,
    tile_slot,
    dense,
    cross_v,
    cross_u,
    cross_bias,
    cotangent,
):
    tables = lax.axis_size("table")
    nodes = lax.axis_size("node")
    tile_count = tile_mult.shape[0]
    block_size = tile_mult.shape[1]
    emb_width = emb_rows.shape[1]
    local_blocks = emb_rows.shape[0] // block_size
    row_blocks = emb_rows.reshape(-1, block_size, emb_width)
    mult_bf = tile_mult.astype(jnp.bfloat16)

    per_node = tile_count // nodes
    meta = jnp.stack([tile_table, tile_slot, tile_rows], axis=1).astype(jnp.bfloat16)
    meta_block = jnp.zeros((nodes, block_size, emb_width), jnp.bfloat16)
    meta_block = meta_block.at[:, :per_node, :3].set(meta.reshape(nodes, per_node, 3))
    outgoing = jnp.concatenate(
        [
            mult_bf.reshape(nodes, per_node, block_size, block_size),
            jnp.broadcast_to(row_blocks[None], (nodes, local_blocks, block_size, emb_width)),
            meta_block[:, None],
        ],
        axis=1,
    )
    incoming = lax.all_to_all(outgoing, "node", split_axis=0, concat_axis=0, tiled=True)
    cross_v, cross_u, incoming = lax.optimization_barrier((cross_v, cross_u, incoming))
    full_v = lax.all_gather(cross_v, "node", axis=0, tiled=True)
    full_u = lax.all_gather(cross_u, "node", axis=0, tiled=True)
    moved_mult = incoming[:, :per_node].reshape(tile_count, block_size, block_size)
    peer_rows = incoming[:, per_node:per_node + local_blocks].reshape(-1, block_size, emb_width)
    moved_meta = incoming[:, -1, :per_node, :3].reshape(tile_count, 3).astype(jnp.int32)

    moved_table = moved_meta[:, 0]
    moved_slot = moved_meta[:, 1]
    sequence = jnp.arange(tile_count, dtype=jnp.int32)
    source = sequence // per_node
    moved_rows = source * local_blocks + moved_meta[:, 2]
    picked = jnp.take(peer_rows, moved_rows, axis=0)
    products = jnp.einsum(
        "kbr,kre->kbe", moved_mult, picked, preferred_element_type=jnp.float32
    ).reshape(tile_count, -1)

    same_table = moved_table[:, None] == moved_table[None, :]
    first = jnp.min(jnp.where(same_table, sequence[None, :], tile_count), axis=1)
    first_slot = jnp.take(moved_slot, first)
    entry = moved_table * DEPTH + (moved_slot != first_slot).astype(jnp.int32)
    entries = tables * DEPTH
    chosen = entry[None, :] == jnp.arange(entries, dtype=jnp.int32)[:, None]
    send_rows = jnp.dot(
        chosen.astype(jnp.float32), products, precision=lax.Precision.HIGHEST,
        preferred_element_type=jnp.float32,
    ).astype(jnp.bfloat16)
    send_slot = jnp.max(jnp.where(chosen, moved_slot[None, :], -1), axis=1)

    slot_rows = jnp.zeros((tables, SLOT_ROWS, emb_width), jnp.bfloat16)
    slot_rows = slot_rows.at[:, 0, :DEPTH].set(send_slot.reshape(tables, DEPTH).astype(jnp.bfloat16))
    outgoing = jnp.concatenate(
        [send_rows.reshape(tables, DEPTH * block_size, emb_width), slot_rows], axis=1
    )
    arrived = lax.all_to_all(outgoing, "table", split_axis=0, concat_axis=0, tiled=True)
    arrived_slot = arrived[:, DEPTH * block_size, :DEPTH].astype(jnp.int32)
    cross_out, returning = owner_work(
        arrived, arrived_slot, dense, full_v, full_u, cross_bias, cotangent
    )
    came_back = lax.all_to_all(returning, "table", split_axis=0, concat_axis=0, tiled=True)
    tile_grad = lax.dot_general(
        chosen.astype(jnp.bfloat16), came_back.reshape(entries, -1), (((0,), (0,)), ((), ())),
        preferred_element_type=jnp.float32,
    ).astype(jnp.bfloat16)
    tile_grad = lax.all_to_all(
        tile_grad.reshape(tile_count, block_size, emb_width),
        "node", split_axis=0, concat_axis=0, tiled=True,
    )
    tile_grads = jnp.einsum(
        "kbr,kbe->kre", mult_bf, tile_grad, preferred_element_type=jnp.float32
    )
    owner_rows = (
        tile_rows[None, :] == jnp.arange(local_blocks, dtype=jnp.int32)[:, None]
    ).astype(jnp.float32)
    emb_grad = jnp.dot(
        owner_rows,
        tile_grads.reshape(tile_count, -1),
        precision=lax.Precision.HIGHEST,
        preferred_element_type=jnp.float32,
    )
    return (cross_out, emb_grad.reshape(-1, emb_width))


def solution(mesh):
    in_specs = (
        P(("node", "table"), None),
        P(("node", "table"), None, None),
        P(("node", "table")),
        P(("node", "table")),
        P(("node", "table")),
        P(("node", "table"), None),
        P("node", None),
        P("node", None),
        P(),
        P(("node", "table"), None),
    )
    out_specs = (P(("node", "table"), None), P(("node", "table"), None))
    return jax.shard_map(body, mesh=mesh, in_specs=in_specs, out_specs=out_specs, check_vma=False)
```

```python
import jax
import jax.numpy as jnp
from jax import lax
from jax.experimental import pallas as pl
from jax.experimental.pallas import tpu as pltpu
from jax.sharding import PartitionSpec as P

FEATURES = 26
DEPTH = 2
SLOT_ROWS = 8
SAMPLE_BLOCKS = 2
BAG_BLOCKS = 52


def combine_kernel(entry_ref, row_ref, incoming_ref, slots_ref, out_ref, acc_ref):
    tiles = entry_ref.shape[0]
    nodes, _, block_size, emb_width = incoming_ref.shape
    per_node = tiles // nodes
    entries = acc_ref.shape[0]
    acc_ref[...] = jnp.zeros_like(acc_ref)

    def add_tile(k, carry):
        source = k // per_node
        block = row_ref[k]
        product = jnp.dot(
            incoming_ref[source, k % per_node],
            incoming_ref[source, per_node + block],
            preferred_element_type=jnp.float32,
        )
        acc_ref[entry_ref[k]] += product
        return carry

    lax.fori_loop(0, tiles, add_tile, 0)

    def store(i, carry):
        rows = pl.ds(pl.multiple_of((i % DEPTH) * block_size, block_size), block_size)
        out_ref[i // DEPTH, rows, :] = acc_ref[i].astype(jnp.bfloat16)
        return carry

    lax.fori_loop(0, entries, store, 0)
    out_ref[:, DEPTH * block_size:, :] = slots_ref[...]


def grad_kernel(row_ref, mult_ref, grad_ref, out_ref):
    out_ref[...] = jnp.zeros_like(out_ref)

    def add_tile(k, carry):
        out_ref[row_ref[k]] += lax.dot_general(
            mult_ref[k], grad_ref[k], (((0,), (0,)), ((), ())), preferred_element_type=jnp.float32
        )
        return carry

    lax.fori_loop(0, mult_ref.shape[0], add_tile, 0)


def cross_kernel(
    slot_ref, arrived_ref, dense_ref, v_ref, u_ref, bias_ref, cot_ref,
    out_ref, ret_ref, pooled_ref, layer_ref, dscale_ref, dlayer_ref, bag_ref,
):
    entries, block_size, emb_width = ret_ref.shape
    bags = pooled_ref.shape[0]
    chunks = layer_ref.shape[1] // emb_width
    f32, bf16 = jnp.float32, jnp.bfloat16

    pooled_ref[...] = jnp.zeros_like(pooled_ref)

    def pool(i, carry):
        slot = slot_ref[i]

        @pl.when(slot >= 0)
        def _():
            rows = pl.ds(pl.multiple_of((i % DEPTH) * block_size, block_size), block_size)
            pooled_ref[slot] += arrived_ref[i // DEPTH, rows, :].astype(f32)

        return carry

    lax.fori_loop(0, entries, pool, 0)
    layer_ref[:, 0:emb_width] = dense_ref[...]
    for bag in range(bags):
        feature, half = divmod(bag, SAMPLE_BLOCKS)
        layer_ref[
            half * block_size:(half + 1) * block_size,
            (feature + 1) * emb_width:(feature + 2) * emb_width,
        ] = pooled_ref[bag].astype(bf16)

    hidden = jnp.dot(layer_ref[...], v_ref[...], preferred_element_type=f32).astype(bf16)

    def forward(c, carry):
        cols = pl.ds(pl.multiple_of(c * emb_width, emb_width), emb_width)
        scale = jnp.dot(hidden, u_ref[:, cols], preferred_element_type=f32) + bias_ref[:, cols]
        layer_input = layer_ref[:, cols].astype(f32)
        upstream = cot_ref[:, cols].astype(f32)
        out_ref[:, cols] = (layer_input * (scale + 1.0)).astype(bf16)
        dscale_ref[:, cols] = (upstream * layer_input).astype(bf16)
        dlayer_ref[:, cols] = upstream * (scale + 1.0)
        return carry

    lax.fori_loop(0, chunks, forward, 0)
    dhidden = lax.dot_general(
        dscale_ref[...], u_ref[...], (((1,), (1,)), ((), ())), preferred_element_type=f32
    ).astype(bf16)

    def backward(feature, carry):
        start = pl.multiple_of((feature + 1) * emb_width, emb_width)
        cols = pl.ds(start, emb_width)
        dlayer = dlayer_ref[:, cols] + lax.dot_general(
            dhidden, v_ref[cols, :], (((1,), (1,)), ((), ())), preferred_element_type=f32
        )
        grad = dlayer.astype(bf16)
        for half in range(SAMPLE_BLOCKS):
            bag_ref[feature * SAMPLE_BLOCKS + half] = grad[half * block_size:(half + 1) * block_size]
        return carry

    lax.fori_loop(0, chunks - 1, backward, 0)

    def gather_back(i, carry):
        slot = slot_ref[i]
        picked = bag_ref[jnp.maximum(slot, 0)]
        ret_ref[i] = jnp.where(slot >= 0, picked, jnp.zeros_like(picked))
        return carry

    lax.fori_loop(0, entries, gather_back, 0)


def owner_work(arrived, arrived_slot, dense, cross_v, cross_u, cross_bias, cotangent):
    emb_width = arrived.shape[-1]
    block_size = emb_width
    entries = arrived.shape[0] * DEPTH
    samples, width = cotangent.shape
    rank = cross_v.shape[1]
    vmem = pl.BlockSpec(memory_space=pltpu.VMEM)
    flops = 8 * samples * width * rank
    nbytes = 2 * (2 * entries * block_size * emb_width + 2 * width * rank + 2 * samples * width)
    cross_out, returning = pl.pallas_call(
        cross_kernel,
        out_shape=(
            jax.ShapeDtypeStruct((samples, width), jnp.bfloat16),
            jax.ShapeDtypeStruct((entries, block_size, emb_width), jnp.bfloat16),
        ),
        in_specs=[pl.BlockSpec(memory_space=pltpu.SMEM)] + [vmem] * 6,
        out_specs=(vmem, vmem),
        scratch_shapes=[
            pltpu.VMEM((BAG_BLOCKS, block_size, emb_width), jnp.float32),
            pltpu.VMEM((samples, width), jnp.bfloat16),
            pltpu.VMEM((samples, width), jnp.bfloat16),
            pltpu.VMEM((samples, width), jnp.float32),
            pltpu.VMEM((BAG_BLOCKS, block_size, emb_width), jnp.bfloat16),
        ],
        compiler_params=pltpu.CompilerParams(vmem_limit_bytes=64 * 1024 * 1024),
        cost_estimate=pl.CostEstimate(flops=flops, bytes_accessed=nbytes, transcendentals=0),
    )(
        arrived_slot.reshape(-1),
        arrived,
        dense,
        cross_v,
        cross_u,
        cross_bias.reshape(1, -1),
        cotangent,
    )
    return cross_out, returning.reshape(-1, DEPTH, block_size, emb_width)


def body(
    emb_rows,
    tile_mult,
    tile_rows,
    tile_table,
    tile_slot,
    dense,
    cross_v,
    cross_u,
    cross_bias,
    cotangent,
):
    tables = lax.axis_size("table")
    nodes = lax.axis_size("node")
    tile_count = tile_mult.shape[0]
    block_size = tile_mult.shape[1]
    emb_width = emb_rows.shape[1]
    local_blocks = emb_rows.shape[0] // block_size
    row_blocks = emb_rows.reshape(-1, block_size, emb_width)
    mult_bf = tile_mult.astype(jnp.bfloat16)

    per_node = tile_count // nodes
    meta = jnp.stack([tile_table, tile_slot, tile_rows], axis=1).astype(jnp.bfloat16)
    meta_block = jnp.zeros((nodes, block_size, emb_width), jnp.bfloat16)
    meta_block = meta_block.at[:, :per_node, :3].set(meta.reshape(nodes, per_node, 3))
    outgoing = jnp.concatenate(
        [
            mult_bf.reshape(nodes, per_node, block_size, block_size),
            jnp.broadcast_to(row_blocks[None], (nodes, local_blocks, block_size, emb_width)),
            meta_block[:, None],
        ],
        axis=1,
    )
    incoming = lax.all_to_all(outgoing, "node", split_axis=0, concat_axis=0, tiled=True)
    cross_v, cross_u, incoming = lax.optimization_barrier((cross_v, cross_u, incoming))
    full_v = lax.all_gather(cross_v, "node", axis=0, tiled=True)
    full_u = lax.all_gather(cross_u, "node", axis=0, tiled=True)
    moved_meta = incoming[:, -1, :per_node, :3].reshape(tile_count, 3).astype(jnp.int32)
    moved_table = moved_meta[:, 0]
    moved_slot = moved_meta[:, 1]
    sequence = jnp.arange(tile_count, dtype=jnp.int32)

    same_table = moved_table[:, None] == moved_table[None, :]
    first = jnp.min(jnp.where(same_table, sequence[None, :], tile_count), axis=1)
    first_slot = jnp.take(moved_slot, first)
    entry = moved_table * DEPTH + (moved_slot != first_slot).astype(jnp.int32)
    entries = tables * DEPTH
    chosen = entry[None, :] == jnp.arange(entries, dtype=jnp.int32)[:, None]
    send_slot = jnp.max(jnp.where(chosen, moved_slot[None, :], -1), axis=1)

    slot_rows = jnp.zeros((tables, SLOT_ROWS, emb_width), jnp.bfloat16)
    slot_rows = slot_rows.at[:, 0, :DEPTH].set(send_slot.reshape(tables, DEPTH).astype(jnp.bfloat16))
    vmem = pl.BlockSpec(memory_space=pltpu.VMEM)
    smem = pl.BlockSpec(memory_space=pltpu.SMEM)
    outgoing = pl.pallas_call(
        combine_kernel,
        out_shape=jax.ShapeDtypeStruct(
            (tables, DEPTH * block_size + SLOT_ROWS, emb_width), jnp.bfloat16
        ),
        in_specs=[smem, smem, vmem, vmem],
        out_specs=vmem,
        scratch_shapes=[pltpu.VMEM((entries, block_size, emb_width), jnp.float32)],
        compiler_params=pltpu.CompilerParams(vmem_limit_bytes=48 * 1024 * 1024),
        cost_estimate=pl.CostEstimate(
            flops=2 * tile_count * block_size ** 3,
            bytes_accessed=2 * (incoming.size + entries * block_size * emb_width),
            transcendentals=0,
        ),
    )(entry, moved_meta[:, 2], incoming, slot_rows)
    arrived = lax.all_to_all(outgoing, "table", split_axis=0, concat_axis=0, tiled=True)
    arrived_slot = arrived[:, DEPTH * block_size, :DEPTH].astype(jnp.int32)
    cross_out, returning = owner_work(
        arrived, arrived_slot, dense, full_v, full_u, cross_bias, cotangent
    )
    came_back = lax.all_to_all(returning, "table", split_axis=0, concat_axis=0, tiled=True)
    tile_grad = lax.dot_general(
        chosen.astype(jnp.bfloat16), came_back.reshape(entries, -1), (((0,), (0,)), ((), ())),
        preferred_element_type=jnp.float32,
    ).astype(jnp.bfloat16)
    tile_grad = lax.all_to_all(
        tile_grad.reshape(tile_count, block_size, emb_width),
        "node", split_axis=0, concat_axis=0, tiled=True,
    )
    emb_grad = pl.pallas_call(
        grad_kernel,
        out_shape=jax.ShapeDtypeStruct((local_blocks, block_size, emb_width), jnp.float32),
        in_specs=[smem, vmem, vmem],
        out_specs=vmem,
        cost_estimate=pl.CostEstimate(
            flops=2 * tile_count * block_size ** 3,
            bytes_accessed=2 * (mult_bf.size + tile_grad.size),
            transcendentals=0,
        ),
    )(tile_rows, mult_bf, tile_grad)
    return (cross_out, emb_grad.reshape(-1, emb_width))


def solution(mesh):
    in_specs = (
        P(("node", "table"), None),
        P(("node", "table"), None, None),
        P(("node", "table")),
        P(("node", "table")),
        P(("node", "table")),
        P(("node", "table"), None),
        P("node", None),
        P("node", None),
        P(),
        P(("node", "table"), None),
    )
    out_specs = (P(("node", "table"), None), P(("node", "table"), None))
    return jax.shard_map(body, mesh=mesh, in_specs=in_specs, out_specs=out_specs, check_vma=False)
```
